32 devices in a mesh: date: 16 (over z, y, core), az: 2 (over x).
Axes of the slice: x: 2, y: 2, z: 4, core: 2. Of those that a mesh axis runs over, the one named last changes fastest.
Arguments:
- raw_stack: float32 [2, 128, 32, 1024], P(None, 'date', None, 'az'), may hold values from -6 to 6
- azimuth_filter: float32 [2, 32, 1024], replicated, may hold values from -6 to 6
- start_vectors: float32 [2, 1024, 32, 128], P(None, 'date', 'az'), may hold values from -6 to 6
- window_offsets: int32 [64, 2, 2], P('date', 'az'), may hold values from -1 to 1
Outputs:
- linked: float32 [2, 1024, 32, 128], P(None, 'date', 'az')
The draws below stay inside these ranges and needn't reach their ends.
All inputs are finite; a program needn't handle non-finite values.
Results may differ from the reference program's by a relative error of at most 0.0003.
Values sent between devices are 32-bit elements; how exact they have to be, the bound alone decides.
A program may use at most 128 MiB of HBM per device.

```python
import math
import jax
import jax.numpy as jnp
from jax import lax

DATES = 128
AZ = 1024
TILE = 16
WIN = 5
ITERS = 8
RANGE = 32


def set_ends(result, own_key, least, top_value):
    longest = result.shape.index(max(result.shape))
    spots = []
    for shift in (0, 1):
        where = [jax.random.randint(jax.random.fold_in(own_key, axis), (), 0, length) for axis, length in enumerate(result.shape)]
        where[longest] = (where[longest] + shift) % result.shape[longest]
        spots.append(tuple(where))
    return result.at[spots[0]].set(least).at[spots[1]].set(top_value)


def block_scale(key, shape, shards, low, high):
    loudness = 1.0
    for position, shards_of in shards:
        steps = jax.random.uniform(jax.random.fold_in(jax.random.fold_in(key, 6), position), (shards_of,), jnp.float32, low / len(shards), high / len(shards))
        loudness = loudness * jnp.repeat(jnp.exp(steps), shape[position] // shards_of).reshape((-1,) + (1,) * (len(shape) - 1 - position))
    return loudness


def noise(own_key, dims, width, reach, pieces=(), kind=jnp.bfloat16):
    result = jax.random.normal(own_key, dims, jnp.float32) * width
    if len(pieces) > 0:
        result = block_scale(own_key, dims, pieces, -0.22, 0.18) * result
    return jnp.clip(result, min=-reach, max=reach).astype(kind)


def setup_inputs(seed: int = 0) -> dict:
    arg_keys = jax.random.split(jax.random.key(seed), 5)
    return {
        "raw_stack": noise(arg_keys[0], (2, DATES, RANGE, AZ), 1.0, 6.0, ((1, 16), (3, 2)), jnp.float32),
        "azimuth_filter": noise(arg_keys[1], (2, RANGE, AZ), 1.0, 6.0, (), jnp.float32),
        "start_vectors": noise(arg_keys[2], (2, AZ, RANGE, DATES), 1.0, 6.0, ((1, 16), (2, 2)), jnp.float32),
        "window_offsets": set_ends(jax.random.randint(arg_keys[3], (AZ // TILE, RANGE // TILE, 2), -1, 2), jax.random.fold_in(arg_keys[3], 1), -1, 1).astype(jnp.int32),
    }


def tables(length):
    index = jnp.arange(length, dtype=jnp.int32)
    phase = index[:, None] * index[None, :] % length
    angle = phase.astype(jnp.float32) * (2.0 * math.pi / length)
    return (jnp.cos(angle), jnp.sin(angle))

def focus(signal, filt):
    cosine, sine = tables(signal.shape[3])
    highest = lax.Precision.HIGHEST

    def forward(field, table):
        return jnp.einsum('dca,ak->dck', field, table, precision=highest)

    def backward(field, table):
        return jnp.einsum('dck,ka->acd', field, table, precision=highest)
    real_in, imag_in = (signal[0], signal[1])
    spec_real = forward(real_in, cosine) + forward(imag_in, sine)
    spec_imag = forward(imag_in, cosine) - forward(real_in, sine)
    filt_real = spec_real * filt[0] - spec_imag * filt[1]
    filt_imag = spec_real * filt[1] + spec_imag * filt[0]
    inverse = 1.0 / signal.shape[3]
    out_real = (backward(filt_real, cosine) - backward(filt_imag, sine)) * inverse
    out_imag = (backward(filt_imag, cosine) + backward(filt_real, sine)) * inverse
    return jnp.stack([out_real, out_imag])

def link(window, start):
    side = start.shape[1]
    real_z, imag_z = (window[0], window[1])
    views = [(real_z[a:a + side, b:b + side], imag_z[a:a + side, b:b + side]) for a in range(WIN) for b in range(WIN)]
    power = jnp.zeros_like(start[0])
    for view_real, view_imag in views:
        power = power + view_real * view_real + view_imag * view_imag
    scale = 1.0 / jnp.sqrt(power + 1e-06)
    vec_real, vec_imag = (start[0], start[1])
    for step in range(ITERS):
        wgt_real, wgt_imag = (vec_real * scale, vec_imag * scale)
        acc_real = jnp.zeros_like(vec_real)
        acc_imag = jnp.zeros_like(vec_imag)
        for view_real, view_imag in views:
            proj_real = lax.optimization_barrier(jnp.sum(view_real * wgt_real + view_imag * wgt_imag, axis=-1, keepdims=True))
            proj_imag = lax.optimization_barrier(jnp.sum(view_real * wgt_imag - view_imag * wgt_real, axis=-1, keepdims=True))
            acc_real = acc_real + view_real * proj_real - view_imag * proj_imag
            acc_imag = acc_imag + view_real * proj_imag + view_imag * proj_real
        gam_real, gam_imag = (acc_real * scale, acc_imag * scale)
        length = jnp.sqrt(lax.optimization_barrier(jnp.sum(gam_real * gam_real + gam_imag * gam_imag, axis=-1, keepdims=True)) + 1e-06)
        vec_real, vec_imag = (gam_real / length, gam_imag / length)
    return jnp.stack([vec_real, vec_imag])

def reference(raw_stack, azimuth_filter, start_vectors, window_offsets):
    focused = focus(raw_stack, azimuth_filter)
    rim = WIN // 2 + 1
    padded = jnp.pad(focused, ((0, 0), (rim, rim), (rim, rim), (0, 0)))
    rows_tiles = AZ // TILE
    cols_tiles = RANGE // TILE
    span = TILE + WIN - 1

    def one_tile(number):
        tile_row = number // cols_tiles
        tile_col = number % cols_tiles
        shift = window_offsets[tile_row, tile_col]
        zero = jnp.zeros((), jnp.int32)
        first_row = (tile_row * TILE + 1 + shift[0]).astype(jnp.int32)
        first_col = (tile_col * TILE + 1 + shift[1]).astype(jnp.int32)
        window = lax.dynamic_slice(padded, (zero, first_row, first_col, zero), (2, span, span, DATES))
        start = lax.dynamic_slice(start_vectors, (zero, (tile_row * TILE).astype(jnp.int32), (tile_col * TILE).astype(jnp.int32), zero), (2, TILE, TILE, DATES))
        return link(window, start)
    results = lax.map(one_tile, jnp.arange(rows_tiles * cols_tiles, dtype=jnp.int32))
    results = results.reshape(rows_tiles, cols_tiles, 2, TILE, TILE, DATES)
    results = jnp.transpose(results, (2, 0, 3, 1, 4, 5))
    return results.reshape(2, AZ, RANGE, DATES)
```

```python
import functools
import math

import jax
import jax.numpy as jnp
import numpy as np
from jax import lax
from jax.experimental import pallas as pl
from jax.experimental.pallas import tpu as pltpu
from jax.sharding import PartitionSpec as P

TILE = 16
WIN = 5
ITERS = 8
RIM = WIN // 2 + 1
HALF = TILE // 2
SPAN_ROWS = HALF + WIN - 1
SPAN_COLS = TILE + WIN - 1
PIXELS = HALF * TILE
USED = SPAN_ROWS * SPAN_COLS
SLOTS = 256
LANES = 128


def parts_of(value):
    high = value.astype(jnp.bfloat16)
    return high, (value - high.astype(jnp.float32)).astype(jnp.bfloat16)


def padded(block, sides, width):
    for axis, dim in sides:
        count = lax.axis_size(axis)
        forward = [(i, i + 1) for i in range(count - 1)]
        backward = [(target, source) for source, target in forward]
        low = lax.ppermute(
            lax.slice_in_dim(block, block.shape[dim] - width, None, axis=dim), axis, forward
        )
        high = lax.ppermute(lax.slice_in_dim(block, 0, width, axis=dim), axis, backward)
        block = jnp.concatenate([low, block, high], axis=dim)
    return block


def butterflies(values, sign):
    count = len(values)
    if count == 1:
        return values
    even = butterflies(values[0::2], sign)
    odd = butterflies(values[1::2], sign)
    low, high = [], []
    for k in range(count // 2):
        (er, ei), (dr, di) = even[k], odd[k]
        if k == 0:
            tr, ti = dr, di
        elif 4 * k == count:
            tr, ti = (-di, dr) if sign > 0 else (di, -dr)
        else:
            c = math.cos(2 * math.pi * k / count)
            s = sign * math.sin(2 * math.pi * k / count)
            tr, ti = dr * c - di * s, dr * s + di * c
        low.append((er + tr, ei + ti))
        high.append((er - tr, ei - ti))
    return low + high


def focus_tables(length):
    radix = length // LANES
    a = np.arange(LANES)
    angle = 2 * np.pi * (np.outer(a, a) % LANES) / LANES
    c, s = np.cos(angle), np.sin(angle)
    forward = np.block([[c, -s], [s, c]])
    backward = np.block([[c, s], [-s, c]])

    def stacked(table):
        high = table.astype(jnp.bfloat16)
        low = (table - high.astype(np.float64)).astype(jnp.bfloat16)
        return np.concatenate([high, high, low], axis=0)

    turn = 2 * np.pi * np.outer(np.arange(radix), a) / length
    twist = np.stack([np.cos(turn), np.sin(turn)]).astype(np.float32)
    return stacked(forward), stacked(backward), twist


def focus_kernel(lines, x_ref, f_ref, fwd_ref, bwd_ref, tw_ref, o_ref):
    rows, length = x_ref.shape[2], x_ref.shape[3]
    radix = length // LANES

    def product(value, table_ref):
        high, low = parts_of(value)
        return jnp.dot(
            jnp.concatenate([high, low, high], axis=1),
            table_ref[...],
            preferred_element_type=jnp.float32,
        )

    cols = [slice(b * LANES, (b + 1) * LANES) for b in range(radix)]
    field = [(x_ref[0, 0, :, c], x_ref[1, 0, :, c]) for c in cols]
    stack = []
    for k, (re, im) in enumerate(butterflies(field, -1)):
        c, s = tw_ref[0, k : k + 1, :], tw_ref[1, k : k + 1, :]
        stack.append(jnp.concatenate([re * c + im * s, im * c - re * s], axis=1))
    spec = product(jnp.concatenate(stack, axis=0), fwd_ref)
    sr, si = spec[:, :LANES], spec[:, LANES:]
    fr = f_ref[0].reshape(radix * rows, LANES)
    fi = f_ref[1].reshape(radix * rows, LANES)
    back = product(jnp.concatenate([sr * fr - si * fi, sr * fi + si * fr], axis=1), bwd_ref)
    inverse = 1.0 / length
    field = []
    for k in range(radix):
        c, s = tw_ref[0, k : k + 1, :] * inverse, tw_ref[1, k : k + 1, :] * inverse
        re = back[k * rows : (k + 1) * rows, :LANES]
        im = back[k * rows : (k + 1) * rows, LANES:]
        field.append((re * c - im * s, im * c + re * s))
    field = butterflies(field, 1)
    for block in range(length // lines):
        b, low = block * lines // LANES, block * lines % LANES
        re, im = field[b]
        o_ref[block, 0] = jnp.concatenate(
            [re[:, low : low + lines], im[:, low : low + lines]], axis=1
        )


def focus(signal, filt, lines):
    _, dates, bins, length = signal.shape
    radix = length // LANES
    forward, backward, twist = focus_tables(length)
    filt = filt.reshape(2, bins, LANES, radix).transpose(0, 3, 1, 2)
    blocks = length // lines
    return pl.pallas_call(
        functools.partial(focus_kernel, lines),
        grid=(dates,),
        in_specs=[
            pl.BlockSpec((2, 1, bins, length), lambda d: (0, d, 0, 0)),
            pl.BlockSpec(filt.shape, lambda d: (0, 0, 0, 0)),
            pl.BlockSpec(forward.shape, lambda d: (0, 0)),
            pl.BlockSpec(backward.shape, lambda d: (0, 0)),
            pl.BlockSpec(twist.shape, lambda d: (0, 0, 0)),
        ],
        out_specs=pl.BlockSpec((blocks, 1, bins, 2 * lines), lambda d: (0, d, 0, 0)),
        out_shape=jax.ShapeDtypeStruct((blocks, dates, bins, 2 * lines), jnp.float32),
        name="focus",
    )(signal, filt, jnp.asarray(forward), jnp.asarray(backward), jnp.asarray(twist))


def turn_kernel(bins, x_ref, o_ref):
    rows, width = x_ref.shape
    dates, lines = rows // bins, width // 2
    for b in range(bins):
        flat = x_ref[pl.ds(b, dates, stride=bins), :].T
        o_ref[0, b] = flat[:lines]
        o_ref[1, b] = flat[lines:]


def turn(blocks, bins):
    rows, width = blocks.shape
    return pl.pallas_call(
        functools.partial(turn_kernel, bins),
        out_shape=jax.ShapeDtypeStruct((2, bins, width // 2, rows // bins), jnp.float32),
        name="turn",
    )(blocks)


def link_kernel(off_ref, z_ref, s_ref, o_ref, win, mat, tam, mask):
    i, j = pl.program_id(0), pl.program_id(1)
    dates = z_ref.shape[3]

    @pl.when((i == 0) & (j == 0))
    def _():
        pixel = lax.broadcasted_iota(jnp.int32, (PIXELS, SLOTS), 0)
        slot = lax.broadcasted_iota(jnp.int32, (PIXELS, SLOTS), 1)
        line, col = pixel // TILE, pixel % TILE
        slot_col = (slot * 171) >> 11
        slot_line = slot - slot_col * SPAN_ROWS
        inside = (slot < USED) & (slot_line >= line) & (slot_line < line + WIN)
        inside = inside & (slot_col >= col) & (slot_col < col + WIN)
        one = jnp.where(inside, 1.0, 0.0)
        mask[...] = jnp.concatenate([one, one], axis=1)

    first_row = i * HALF + 1 + off_ref[i // 2, j, 0]
    first_col = j * TILE + 1 + off_ref[i // 2, j, 1]
    for c in range(2):
        for b in range(SPAN_COLS):
            win[c, b * SPAN_ROWS : (b + 1) * SPAN_ROWS, :] = z_ref[
                c, first_col + b, pl.ds(first_row, SPAN_ROWS), :
            ]
        win[c, USED:SLOTS, :] = jnp.zeros((SLOTS - USED, dates), jnp.float32)
    zr, zi = win[0], win[1]
    high, low = parts_of(zr * zr + zi * zi)
    picks = mask[...].astype(jnp.bfloat16)
    power = jnp.dot(picks, jnp.concatenate([high, low], axis=0), preferred_element_type=jnp.float32)
    scale = 1.0 / jnp.sqrt(power + 1e-06)
    scale = jnp.concatenate([scale, scale], axis=1)

    whole = jnp.concatenate(
        [jnp.concatenate([zr, zi], axis=1), jnp.concatenate([-zi, zr], axis=1)], axis=0
    )
    high, low = parts_of(whole)
    mat[...] = jnp.concatenate([high, high, low], axis=0)
    tr, ti = zr.T, zi.T
    high, low = parts_of(
        jnp.concatenate(
            [jnp.concatenate([tr, -ti], axis=1), jnp.concatenate([ti, tr], axis=1)], axis=0
        )
    )
    tam[...] = jnp.concatenate([high, high, low], axis=0)

    vec = jnp.concatenate(
        [s_ref[0].reshape(PIXELS, dates), s_ref[1].reshape(PIXELS, dates)], axis=1
    )

    def product(value, table_ref):
        high, low = parts_of(value)
        return jnp.dot(
            jnp.concatenate([high, low, high], axis=1),
            table_ref[...],
            preferred_element_type=jnp.float32,
        )

    for step in range(ITERS):
        proj = product(vec * scale, tam) * mask[...]
        gam = product(proj, mat) * scale
        length = jnp.sqrt(jnp.sum(gam * gam, axis=1, keepdims=True) + 1e-06)
        vec = gam / length
    o_ref[0] = vec[:, :dates].reshape(HALF, TILE, dates)
    o_ref[1] = vec[:, dates:].reshape(HALF, TILE, dates)


def link(window, starts, shifts):
    _, lines, bins, dates = starts.shape
    spec = pl.BlockSpec((2, HALF, TILE, dates), lambda i, j, off: (0, i, j, 0))
    return pl.pallas_call(
        link_kernel,
        grid_spec=pltpu.PrefetchScalarGridSpec(
            num_scalar_prefetch=1,
            grid=(lines // HALF, bins // TILE),
            in_specs=[pl.BlockSpec(window.shape, lambda i, j, off: (0, 0, 0, 0)), spec],
            out_specs=spec,
            scratch_shapes=[
                pltpu.VMEM((2, SLOTS, dates), jnp.float32),
                pltpu.VMEM((6 * SLOTS, 2 * dates), jnp.bfloat16),
                pltpu.VMEM((6 * dates, 2 * SLOTS), jnp.bfloat16),
                pltpu.VMEM((PIXELS, 2 * SLOTS), jnp.float32),
            ],
        ),
        out_shape=jax.ShapeDtypeStruct(starts.shape, jnp.float32),
        name="link",
    )(shifts, window, starts)


def shards(raw_stack, azimuth_filter, start_vectors, window_offsets):
    az_parts = lax.axis_size("az")
    date_parts = lax.axis_size("date")
    bins = raw_stack.shape[2] // az_parts
    lines = raw_stack.shape[3] * az_parts // date_parts
    turned = lax.all_to_all(raw_stack, "az", split_axis=2, concat_axis=3, tiled=True)
    filt_part = lax.dynamic_slice_in_dim(azimuth_filter, lax.axis_index("az") * bins, bins, 1)
    blocks = focus(turned, filt_part, lines)
    blocks = lax.all_to_all(blocks, "date", split_axis=0, concat_axis=0, tiled=True)
    flat = turn(blocks.reshape(-1, 2 * lines), bins)
    window = padded(flat, (("date", 2), ("az", 1)), RIM)
    return link(window, start_vectors, window_offsets)


def solution(mesh):
    placed = (P(None, "date", None, "az"), P(), P(None, "date", "az", None), P("date", "az", None))
    return jax.shard_map(
        shards, mesh=mesh, in_specs=placed, out_specs=P(None, "date", "az", None), check_vma=False
    )
```

```python
import functools
import math

import jax
import jax.numpy as jnp
import numpy as np
from jax import lax
from jax.experimental import pallas as pl
from jax.experimental.pallas import tpu as pltpu
from jax.sharding import PartitionSpec as P

TILE = 16
WIN = 5
ITERS = 8
RIM = WIN // 2 + 1
HALF = TILE // 2
SPAN_ROWS = HALF + WIN - 1
SPAN_COLS = TILE + WIN - 1
PIXELS = HALF * TILE
USED = SPAN_ROWS * SPAN_COLS
SLOTS = 256
LANES = 128
GROUP = 4
STACKED = False


def parts_of(value):
    high = value.astype(jnp.bfloat16)
    return high, (value - high.astype(jnp.float32)).astype(jnp.bfloat16)


def butterflies(values, sign):
    count = len(values)
    if count == 1:
        return values
    even = butterflies(values[0::2], sign)
    odd = butterflies(values[1::2], sign)
    low, high = [], []
    for k in range(count // 2):
        (er, ei), (dr, di) = even[k], odd[k]
        if k == 0:
            tr, ti = dr, di
        elif 4 * k == count:
            tr, ti = (-di, dr) if sign > 0 else (di, -dr)
        else:
            c = math.cos(2 * math.pi * k / count)
            s = sign * math.sin(2 * math.pi * k / count)
            tr, ti = dr * c - di * s, dr * s + di * c
        low.append((er + tr, ei + ti))
        high.append((er - tr, ei - ti))
    return low + high


def focus_tables(length):
    radix = length // LANES
    a = np.arange(LANES)
    angle = 2 * np.pi * (np.outer(a, a) % LANES) / LANES
    c, s = np.cos(angle), np.sin(angle)
    forward = np.block([[c, -s], [s, c]])
    backward = np.block([[c, s], [-s, c]])

    def stacked(table):
        high = table.astype(jnp.bfloat16)
        low = (table - high.astype(np.float64)).astype(jnp.bfloat16)
        return np.concatenate([high, high, low], axis=0)

    turn = 2 * np.pi * np.outer(np.arange(radix), a) / length
    twist = np.stack([np.cos(turn), np.sin(turn)]).astype(np.float32)
    return stacked(forward), stacked(backward), twist


def neighbours():
    return [(dd, da) for dd in (-1, 0, 1) for da in (-1, 0, 1) if (dd, da) != (0, 0)]


def exchange_kernel(
    date_parts, az_parts, chunk,
    raw_ref, f_ref, fwd_ref, bwd_ref, tw_ref, z_ref,
    inbox, outbox, mailbox,
    own_sem, az_send, az_recv, date_send, date_recv, rim_send, rim_recv,
):
    _, dates, all_bins, width = raw_ref.shape
    bins = all_bins // az_parts
    length = width * az_parts
    lines = length // date_parts
    radix = length // LANES
    chunks = dates // chunk
    rows = chunk * bins
    block = dates * bins
    my_date, my_az = lax.axis_index("date"), lax.axis_index("az")

    def inside(dd, da):
        date, az = my_date + dd, my_az + da
        return (date >= 0) & (date < date_parts) & (az >= 0) & (az < az_parts)

    def device(date, az):
        return {"date": date, "az": az}

    z_ref[...] = jnp.zeros_like(z_ref)
    barrier = pltpu.get_barrier_semaphore()
    mesh_ids = pl.DeviceIdType.MESH
    expected = date_parts - 1 + az_parts - 1
    for k in range(1, date_parts):
        peer = lax.rem(my_date + k, date_parts)
        pl.semaphore_signal(barrier, inc=1, device_id=device(peer, my_az), device_id_type=mesh_ids)
    for k in range(1, az_parts):
        peer = lax.rem(my_az + k, az_parts)
        pl.semaphore_signal(barrier, inc=1, device_id=device(my_date, peer), device_id_type=mesh_ids)
    for dd, da in neighbours():
        if dd != 0 and da != 0:
            there = inside(dd, da)
            expected = expected + there.astype(jnp.int32)

            @pl.when(there)
            def _():
                pl.semaphore_signal(
                    barrier,
                    inc=1,
                    device_id=device(my_date + dd, my_az + da),
                    device_id_type=mesh_ids,
                )

    pl.semaphore_wait(barrier, expected)

    def az_copy(step, peer):
        return pltpu.make_async_remote_copy(
            src_ref=raw_ref.at[
                :, pl.ds(step * chunk, chunk), pl.ds(pl.multiple_of(peer * bins, 8), bins), :
            ],
            dst_ref=inbox.at[my_az, :, pl.ds(step * chunk, chunk)],
            send_sem=az_send.at[step, peer],
            recv_sem=az_recv.at[step, my_az],
            device_id=device(my_date, peer),
            device_id_type=mesh_ids,
        )

    def az_arrival(step, peer):
        return pltpu.make_async_remote_copy(
            src_ref=raw_ref.at[:, pl.ds(step * chunk, chunk), pl.ds(0, bins), :],
            dst_ref=inbox.at[peer, :, pl.ds(step * chunk, chunk)],
            send_sem=az_send.at[step, peer],
            recv_sem=az_recv.at[step, peer],
            device_id=device(my_date, peer),
            device_id_type=mesh_ids,
        )

    for step in range(chunks):
        for k in range(1, az_parts):
            az_copy(step, lax.rem(my_az + k, az_parts)).start()
    own = pltpu.make_async_copy(
        raw_ref.at[:, :, pl.ds(pl.multiple_of(my_az * bins, 8), bins), :],
        inbox.at[my_az],
        own_sem.at[0],
    )
    own.start()
    own.wait()

    def product(value, table_ref):
        high, low = parts_of(value)
        return jnp.dot(
            jnp.concatenate([high, low, high], axis=1),
            table_ref[...],
            preferred_element_type=jnp.float32,
        )

    def date_copy(peer, start, size):
        return pltpu.make_async_remote_copy(
            src_ref=outbox.at[peer, pl.ds(start, size), :],
            dst_ref=mailbox.at[pl.ds(pl.multiple_of(my_date * block + start, 8), size), :],
            send_sem=date_send.at[peer],
            recv_sem=date_recv.at[my_date],
            device_id=device(peer, my_az),
            device_id_type=mesh_ids,
        )

    def date_arrival(peer):
        return pltpu.make_async_remote_copy(
            src_ref=outbox.at[peer],
            dst_ref=mailbox.at[pl.ds(pl.multiple_of(peer * block, 8), block), :],
            send_sem=date_send.at[peer],
            recv_sem=date_recv.at[peer],
            device_id=device(peer, my_az),
            device_id_type=mesh_ids,
        )

    @pl.loop(0, chunks)
    def _(step):
        for k in range(1, az_parts):
            az_arrival(step, lax.rem(my_az + k, az_parts)).wait_recv()
        field = []
        for b in range(radix):
            source, at = b * LANES // width, b * LANES % width
            field.append(
                tuple(
                    inbox[source, c, pl.ds(step * chunk, chunk), :, at : at + LANES].reshape(
                        rows, LANES
                    )
                    for c in range(2)
                )
            )
        stack = []
        for k, (re, im) in enumerate(butterflies(field, -1)):
            c, s = tw_ref[0, k : k + 1, :], tw_ref[1, k : k + 1, :]
            stack.append(jnp.concatenate([re * c + im * s, im * c - re * s], axis=1))
        spec = product(jnp.concatenate(stack, axis=0), fwd_ref)
        sr, si = spec[:, :LANES], spec[:, LANES:]
        full = (radix, chunk, bins, LANES)
        fr = jnp.broadcast_to(f_ref[0][:, None], full).reshape(radix * rows, LANES)
        fi = jnp.broadcast_to(f_ref[1][:, None], full).reshape(radix * rows, LANES)
        back = product(jnp.concatenate([sr * fr - si * fi, sr * fi + si * fr], axis=1), bwd_ref)
        inverse = 1.0 / length
        field = []
        for k in range(radix):
            c, s = tw_ref[0, k : k + 1, :] * inverse, tw_ref[1, k : k + 1, :] * inverse
            re = back[k * rows : (k + 1) * rows, :LANES]
            im = back[k * rows : (k + 1) * rows, LANES:]
            field.append((re * c - im * s, im * c + re * s))
        field = butterflies(field, 1)
        start = pl.multiple_of(step * rows, 8)
        for place in range(date_parts):
            b, low = place * lines // LANES, place * lines % LANES
            re, im = field[b]
            outbox[place, pl.ds(start, rows), :] = jnp.concatenate(
                [re[:, low : low + lines], im[:, low : low + lines]], axis=1
            )
        for k in range(1, date_parts):
            date_copy(lax.rem(my_date + k, date_parts), start, rows).start()

    keep = pltpu.make_async_copy(
        outbox.at[my_date],
        mailbox.at[pl.ds(pl.multiple_of(my_date * block, 8), block), :],
        own_sem.at[1],
    )
    keep.start()
    keep.wait()
    for k in range(1, date_parts):
        date_arrival(lax.rem(my_date + k, date_parts)).wait_recv()

    def rim_copy(n, dd, da):
        lines_at = {-1: (8, 8 + lines, 8), 0: (8, 8, lines), 1: (lines, 0, 8)}[dd]
        bins_at = {-1: (RIM, RIM + bins, RIM), 0: (RIM, RIM, bins), 1: (bins, 0, RIM)}[da]
        return pltpu.make_async_remote_copy(
            src_ref=z_ref.at[:, pl.ds(bins_at[0], bins_at[2]), pl.ds(lines_at[0], lines_at[2]), :],
            dst_ref=z_ref.at[:, pl.ds(bins_at[1], bins_at[2]), pl.ds(lines_at[1], lines_at[2]), :],
            send_sem=rim_send.at[n],
            recv_sem=rim_recv.at[n],
            device_id=device(my_date + dd, my_az + da),
            device_id_type=mesh_ids,
        )

    def send_rims(side):
        for n, (dd, da) in enumerate(neighbours()):
            if da == side:

                @pl.when(inside(dd, da))
                def _():
                    rim_copy(n, dd, da).start()

    edge = list(range(RIM)) + list(range(bins - RIM, bins)) + list(range(RIM, bins - RIM))
    for count, b in enumerate(edge):
        flat = mailbox[pl.ds(b, date_parts * dates, stride=bins), :].T
        z_ref[0, RIM + b, 8 : 8 + lines, :] = flat[:lines]
        z_ref[1, RIM + b, 8 : 8 + lines, :] = flat[lines:]
        if count == RIM - 1:
            send_rims(-1)
        if count == 2 * RIM - 1:
            send_rims(1)
    send_rims(0)

    for step in range(chunks):
        for k in range(1, az_parts):
            az_copy(step, lax.rem(my_az + k, az_parts)).wait_send()
    for k in range(1, date_parts):
        date_arrival(lax.rem(my_date + k, date_parts)).wait_send()
    for n, (dd, da) in enumerate(neighbours()):

        @pl.when(inside(dd, da))
        def _():
            rim_copy(n, dd, da).wait_send()

        @pl.when(inside(-dd, -da))
        def _():
            rim_copy(n, dd, da).wait_recv()


def exchange(raw, filt):
    az_parts, date_parts = lax.axis_size("az"), lax.axis_size("date")
    _, dates, all_bins, width = raw.shape
    bins, length = all_bins // az_parts, width * az_parts
    lines, radix = length // date_parts, length // LANES
    chunk = 2 if dates % 2 == 0 else 1
    forward, backward, twist = focus_tables(length)
    filt = filt.reshape(2, bins, LANES, radix).transpose(0, 3, 1, 2)
    near = pl.BlockSpec(memory_space=pltpu.VMEM)
    dma = pltpu.SemaphoreType.DMA
    return pl.pallas_call(
        functools.partial(exchange_kernel, date_parts, az_parts, chunk),
        in_specs=[pl.BlockSpec(memory_space=pl.ANY)] + [near] * 4,
        out_specs=near,
        out_shape=jax.ShapeDtypeStruct(
            (2, bins + 2 * RIM, lines + 16, date_parts * dates), jnp.float32
        ),
        scratch_shapes=[
            pltpu.VMEM((az_parts, 2, dates, bins, width), jnp.float32),
            pltpu.VMEM((date_parts, dates * bins, 2 * lines), jnp.float32),
            pltpu.VMEM((date_parts * dates * bins, 2 * lines), jnp.float32),
            dma((2,)),
            dma((dates // chunk, az_parts)),
            dma((dates // chunk, az_parts)),
            dma((date_parts,)),
            dma((date_parts,)),
            dma((8,)),
            dma((8,)),
        ],
        compiler_params=pltpu.CompilerParams(
            collective_id=0, has_side_effects=True, vmem_limit_bytes=40 * 1024 * 1024
        ),
        name="exchange",
    )(raw, filt, jnp.asarray(forward), jnp.asarray(backward), jnp.asarray(twist))


def link_kernel(off_ref, z_ref, s_ref, o_ref, win, mat, tam, mask):
    i, j = pl.program_id(0), pl.program_id(1)
    dates = z_ref.shape[3]

    @pl.when((i == 0) & (j == 0))
    def _():
        pixel = lax.broadcasted_iota(jnp.int32, (PIXELS, SLOTS), 0)
        slot = lax.broadcasted_iota(jnp.int32, (PIXELS, SLOTS), 1)
        line, col = pixel // TILE, pixel % TILE
        slot_col = (slot * 171) >> 11
        slot_line = slot - slot_col * SPAN_ROWS
        inside = (slot < USED) & (slot_line >= line) & (slot_line < line + WIN)
        inside = inside & (slot_col >= col) & (slot_col < col + WIN)
        one = jnp.where(inside, 1.0, 0.0)
        mask[...] = jnp.concatenate([one, one], axis=1)

    def product(value, table_ref):
        high, low = parts_of(value)
        if STACKED:
            rows, depth = value.shape
            both = jnp.dot(
                jnp.concatenate([high, low], axis=0),
                table_ref[:depth],
                preferred_element_type=jnp.float32,
            )
            rest = jnp.dot(high, table_ref[depth:], preferred_element_type=jnp.float32)
            return both[:rows] + (both[rows:] + rest)
        return jnp.dot(
            jnp.concatenate([high, low, high], axis=1),
            table_ref[...],
            preferred_element_type=jnp.float32,
        )

    def stacked(high, low):
        return jnp.concatenate([high, low] if STACKED else [high, high, low], axis=0)

    vecs, scales = [], []
    for g in range(GROUP):
        number = i * GROUP + g
        first_row = number * HALF + 9 - RIM + off_ref[number // 2, j, 0]
        first_col = j * TILE + 1 + off_ref[number // 2, j, 1]
        for c in range(2):
            for b in range(SPAN_COLS):
                win[g, c, b * SPAN_ROWS : (b + 1) * SPAN_ROWS, :] = z_ref[
                    c, first_col + b, pl.ds(first_row, SPAN_ROWS), :
                ]
            win[g, c, USED:SLOTS, :] = jnp.zeros((SLOTS - USED, dates), jnp.float32)
        zr, zi = win[g, 0], win[g, 1]
        picks = mask[...].astype(jnp.bfloat16)
        power = jnp.dot(
            picks,
            jnp.concatenate(parts_of(zr * zr + zi * zi), axis=0),
            preferred_element_type=jnp.float32,
        )
        scale = 1.0 / jnp.sqrt(power + 1e-06)
        scales.append(jnp.concatenate([scale, scale], axis=1))

        whole = jnp.concatenate(
            [jnp.concatenate([zr, zi], axis=1), jnp.concatenate([-zi, zr], axis=1)], axis=0
        )
        mat[g] = stacked(*parts_of(whole))
        tr, ti = zr.T, zi.T
        whole = jnp.concatenate(
            [jnp.concatenate([tr, -ti], axis=1), jnp.concatenate([ti, tr], axis=1)], axis=0
        )
        tam[g] = stacked(*parts_of(whole))
        rows = slice(g * HALF, (g + 1) * HALF)
        vecs.append(
            jnp.concatenate(
                [s_ref[0, rows].reshape(PIXELS, dates), s_ref[1, rows].reshape(PIXELS, dates)],
                axis=1,
            )
        )

    for step in range(ITERS):
        projs = [product(vecs[g] * scales[g], tam.at[g]) * mask[...] for g in range(GROUP)]
        for g in range(GROUP):
            gam = product(projs[g], mat.at[g]) * scales[g]
            total = jnp.sum(gam * gam, axis=1, keepdims=True) + 1e-06
            vecs[g] = gam * (1.0 / jnp.sqrt(total))
    for g in range(GROUP):
        rows = slice(g * HALF, (g + 1) * HALF)
        o_ref[0, rows] = vecs[g][:, :dates].reshape(HALF, TILE, dates)
        o_ref[1, rows] = vecs[g][:, dates:].reshape(HALF, TILE, dates)


def link(window, starts, shifts):
    _, lines, bins, dates = starts.shape
    copies = 2 if STACKED else 3
    spec = pl.BlockSpec((2, GROUP * HALF, TILE, dates), lambda i, j, off: (0, i, j, 0))
    return pl.pallas_call(
        link_kernel,
        grid_spec=pltpu.PrefetchScalarGridSpec(
            num_scalar_prefetch=1,
            grid=(lines // (GROUP * HALF), bins // TILE),
            in_specs=[pl.BlockSpec(window.shape, lambda i, j, off: (0, 0, 0, 0)), spec],
            out_specs=spec,
            scratch_shapes=[
                pltpu.VMEM((GROUP, 2, SLOTS, dates), jnp.float32),
                pltpu.VMEM((GROUP, copies * 2 * SLOTS, 2 * dates), jnp.bfloat16),
                pltpu.VMEM((GROUP, copies * 2 * dates, 2 * SLOTS), jnp.bfloat16),
                pltpu.VMEM((PIXELS, 2 * SLOTS), jnp.float32),
            ],
        ),
        out_shape=jax.ShapeDtypeStruct(starts.shape, jnp.float32),
        compiler_params=pltpu.CompilerParams(vmem_limit_bytes=40 * 1024 * 1024),
        name="link",
    )(shifts, window, starts)


def shards(raw_stack, azimuth_filter, start_vectors, window_offsets):
    bins = raw_stack.shape[2] // lax.axis_size("az")
    filt_part = lax.dynamic_slice_in_dim(azimuth_filter, lax.axis_index("az") * bins, bins, 1)
    window = exchange(raw_stack, filt_part)
    return link(window, start_vectors, window_offsets)


def solution(mesh):
    placed = (P(None, "date", None, "az"), P(), P(None, "date", "az", None), P("date", "az", None))
    return jax.shard_map(
        shards, mesh=mesh, in_specs=placed, out_specs=P(None, "date", "az", None), check_vma=False
    )
```

```python
import functools
import math

import jax
import jax.numpy as jnp
import numpy as np
from jax import lax
from jax.experimental import pallas as pl
from jax.experimental.pallas import tpu as pltpu
from jax.sharding import PartitionSpec as P

TILE = 16
WIN = 5
ITERS = 8
RIM = WIN // 2 + 1
HALF = TILE // 2
SPAN_ROWS = HALF + WIN - 1
SPAN_COLS = TILE + WIN - 1
PIXELS = HALF * TILE
USED = SPAN_ROWS * SPAN_COLS
SLOTS = 256
LANES = 128
GROUP = 4
STACKED = False


def parts_of(value):
    high = value.astype(jnp.bfloat16)
    return high, (value - high.astype(jnp.float32)).astype(jnp.bfloat16)


def butterflies(values, sign):
    count = len(values)
    if count == 1:
        return values
    even = butterflies(values[0::2], sign)
    odd = butterflies(values[1::2], sign)
    low, high = [], []
    for k in range(count // 2):
        (er, ei), (dr, di) = even[k], odd[k]
        if k == 0:
            tr, ti = dr, di
        elif 4 * k == count:
            tr, ti = (-di, dr) if sign > 0 else (di, -dr)
        else:
            c = math.cos(2 * math.pi * k / count)
            s = sign * math.sin(2 * math.pi * k / count)
            tr, ti = dr * c - di * s, dr * s + di * c
        low.append((er + tr, ei + ti))
        high.append((er - tr, ei - ti))
    return low + high


def focus_tables(length):
    radix = length // LANES
    a = np.arange(LANES)
    angle = 2 * np.pi * (np.outer(a, a) % LANES) / LANES
    c, s = np.cos(angle), np.sin(angle)
    forward = np.block([[c, -s], [s, c]])
    backward = np.block([[c, s], [-s, c]])

    def stacked(table):
        high = table.astype(jnp.bfloat16)
        low = (table - high.astype(np.float64)).astype(jnp.bfloat16)
        return np.concatenate([high, high, low], axis=0)

    turn = 2 * np.pi * np.outer(np.arange(radix), a) / length
    twist = np.stack([np.cos(turn), np.sin(turn)]).astype(np.float32)
    return stacked(forward), stacked(backward), twist


def neighbours():
    return [(dd, da) for dd in (-1, 0, 1) for da in (-1, 0, 1) if (dd, da) != (0, 0)]


def exchange_kernel(
    date_parts, az_parts, chunk,
    raw_ref, f_ref, fwd_ref, bwd_ref, tw_ref, z_ref,
    inbox, outbox, mailbox, rim_out, rim_in,
    own_sem, az_send, az_recv, date_send, date_recv, rim_send, rim_recv, x_send, x_recv,
):
    _, dates, all_bins, width = raw_ref.shape
    bins = all_bins // az_parts
    length = width * az_parts
    lines = length // date_parts
    radix = length // LANES
    chunks = dates // chunk
    rows = chunk * bins
    block = dates * bins
    my_date, my_az = lax.axis_index("date"), lax.axis_index("az")

    def inside(dd, da):
        date, az = my_date + dd, my_az + da
        return (date >= 0) & (date < date_parts) & (az >= 0) & (az < az_parts)

    def device(date, az):
        return {"date": date, "az": az}

    z_ref[...] = jnp.zeros_like(z_ref)
    barrier = pltpu.get_barrier_semaphore()
    mesh_ids = pl.DeviceIdType.MESH
    expected = date_parts - 1 + az_parts - 1
    for k in range(1, date_parts):
        peer = lax.rem(my_date + k, date_parts)
        pl.semaphore_signal(barrier, inc=1, device_id=device(peer, my_az), device_id_type=mesh_ids)
    for k in range(1, az_parts):
        peer = lax.rem(my_az + k, az_parts)
        pl.semaphore_signal(barrier, inc=1, device_id=device(my_date, peer), device_id_type=mesh_ids)
    for dd, da in neighbours():
        if dd != 0 and da != 0:
            there = inside(dd, da)
            expected = expected + there.astype(jnp.int32)

            @pl.when(there)
            def _():
                pl.semaphore_signal(
                    barrier,
                    inc=1,
                    device_id=device(my_date + dd, my_az + da),
                    device_id_type=mesh_ids,
                )

    pl.semaphore_wait(barrier, expected)

    def az_copy(step, peer):
        return pltpu.make_async_remote_copy(
            src_ref=raw_ref.at[
                :, pl.ds(step * chunk, chunk), pl.ds(pl.multiple_of(peer * bins, 8), bins), :
            ],
            dst_ref=inbox.at[my_az, :, pl.ds(step * chunk, chunk)],
            send_sem=az_send.at[step, peer],
            recv_sem=az_recv.at[step, my_az],
            device_id=device(my_date, peer),
            device_id_type=mesh_ids,
        )

    def az_arrival(step, peer):
        return pltpu.make_async_remote_copy(
            src_ref=raw_ref.at[:, pl.ds(step * chunk, chunk), pl.ds(0, bins), :],
            dst_ref=inbox.at[peer, :, pl.ds(step * chunk, chunk)],
            send_sem=az_send.at[step, peer],
            recv_sem=az_recv.at[step, peer],
            device_id=device(my_date, peer),
            device_id_type=mesh_ids,
        )

    for step in range(chunks):
        for k in range(1, az_parts):
            az_copy(step, lax.rem(my_az + k, az_parts)).start()
    own = pltpu.make_async_copy(
        raw_ref.at[:, :, pl.ds(pl.multiple_of(my_az * bins, 8), bins), :],
        inbox.at[my_az],
        own_sem.at[0],
    )
    own.start()
    own.wait()

    def product(value, table_ref):
        high, low = parts_of(value)
        return jnp.dot(
            jnp.concatenate([high, low, high], axis=1),
            table_ref[...],
            preferred_element_type=jnp.float32,
        )

    def date_copy(peer, start, size):
        return pltpu.make_async_remote_copy(
            src_ref=outbox.at[peer, pl.ds(start, size), :],
            dst_ref=mailbox.at[pl.ds(pl.multiple_of(my_date * block + start, 8), size), :],
            send_sem=date_send.at[peer],
            recv_sem=date_recv.at[my_date],
            device_id=device(peer, my_az),
            device_id_type=mesh_ids,
        )

    def date_arrival(peer):
        return pltpu.make_async_remote_copy(
            src_ref=outbox.at[peer],
            dst_ref=mailbox.at[pl.ds(pl.multiple_of(peer * block, 8), block), :],
            send_sem=date_send.at[peer],
            recv_sem=date_recv.at[peer],
            device_id=device(peer, my_az),
            device_id_type=mesh_ids,
        )

    @pl.loop(0, chunks)
    def _(step):
        for k in range(1, az_parts):
            az_arrival(step, lax.rem(my_az + k, az_parts)).wait_recv()
        field = []
        for b in range(radix):
            source, at = b * LANES // width, b * LANES % width
            field.append(
                tuple(
                    inbox[source, c, pl.ds(step * chunk, chunk), :, at : at + LANES].reshape(
                        rows, LANES
                    )
                    for c in range(2)
                )
            )
        stack = []
        for k, (re, im) in enumerate(butterflies(field, -1)):
            c, s = tw_ref[0, k : k + 1, :], tw_ref[1, k : k + 1, :]
            stack.append(jnp.concatenate([re * c + im * s, im * c - re * s], axis=1))
        spec = product(jnp.concatenate(stack, axis=0), fwd_ref)
        sr, si = spec[:, :LANES], spec[:, LANES:]
        full = (radix, chunk, bins, LANES)
        fr = jnp.broadcast_to(f_ref[0][:, None], full).reshape(radix * rows, LANES)
        fi = jnp.broadcast_to(f_ref[1][:, None], full).reshape(radix * rows, LANES)
        back = product(jnp.concatenate([sr * fr - si * fi, sr * fi + si * fr], axis=1), bwd_ref)
        inverse = 1.0 / length
        field = []
        for k in range(radix):
            c, s = tw_ref[0, k : k + 1, :] * inverse, tw_ref[1, k : k + 1, :] * inverse
            re = back[k * rows : (k + 1) * rows, :LANES]
            im = back[k * rows : (k + 1) * rows, LANES:]
            field.append((re * c - im * s, im * c + re * s))
        field = butterflies(field, 1)
        start = pl.multiple_of(step * rows, 8)
        for place in range(date_parts):
            b, low = place * lines // LANES, place * lines % LANES
            re, im = field[b]
            outbox[place, pl.ds(start, rows), :] = jnp.concatenate(
                [re[:, low : low + lines], im[:, low : low + lines]], axis=1
            )
        for k in range(1, date_parts):
            date_copy(lax.rem(my_date + k, date_parts), start, rows).start()

    keep = pltpu.make_async_copy(
        outbox.at[my_date],
        mailbox.at[pl.ds(pl.multiple_of(my_date * block, 8), block), :],
        own_sem.at[1],
    )
    keep.start()

    def side_copy(side, out, into, landing):
        return pltpu.make_async_remote_copy(
            src_ref=out,
            dst_ref=into,
            send_sem=x_send.at[side],
            recv_sem=x_recv.at[landing],
            device_id=device(my_date, my_az + 2 * side - 1),
            device_id_type=mesh_ids,
        )

    def forward(source):
        for side in range(2):

            @pl.when(inside(0, 2 * side - 1))
            def _():
                for n in range(RIM):
                    b = n + side * (bins - RIM)
                    rim_out[side, source, n * dates : (n + 1) * dates, :] = mailbox[
                        pl.ds(source * block + b, dates, stride=bins), :
                    ]
                side_copy(
                    side, rim_out.at[side, source], rim_in.at[1 - side, source], 1 - side
                ).start()

    keep.wait()
    forward(my_date)
    for k in range(1, date_parts):
        shift = (k + 1) // 2 if k % 2 else date_parts - k // 2
        peer = lax.rem(my_date + shift, date_parts)
        date_arrival(peer).wait_recv()
        forward(peer)

    def rim_copy(n, dd, da):
        lines_at = {-1: (8, 8 + lines, 8), 0: (8, 8, lines), 1: (lines, 0, 8)}[dd]
        bins_at = {-1: (RIM, RIM + bins, RIM), 0: (RIM, RIM, bins), 1: (bins, 0, RIM)}[da]
        return pltpu.make_async_remote_copy(
            src_ref=z_ref.at[:, pl.ds(bins_at[0], bins_at[2]), pl.ds(lines_at[0], lines_at[2]), :],
            dst_ref=z_ref.at[:, pl.ds(bins_at[1], bins_at[2]), pl.ds(lines_at[1], lines_at[2]), :],
            send_sem=rim_send.at[n],
            recv_sem=rim_recv.at[n],
            device_id=device(my_date + dd, my_az + da),
            device_id_type=mesh_ids,
        )

    def send_rims(side):
        for n, (dd, da) in enumerate(neighbours()):
            if da == side and dd != 0:

                @pl.when(inside(dd, da))
                def _():
                    rim_copy(n, dd, da).start()

    edge = list(range(RIM)) + list(range(bins - RIM, bins)) + list(range(RIM, bins - RIM))
    for count, b in enumerate(edge):
        flat = mailbox[pl.ds(b, date_parts * dates, stride=bins), :].T
        z_ref[0, RIM + b, 8 : 8 + lines, :] = flat[:lines]
        z_ref[1, RIM + b, 8 : 8 + lines, :] = flat[lines:]
        if count == RIM - 1:
            send_rims(-1)
        if count == 2 * RIM - 1:
            send_rims(1)
    send_rims(0)
    for side in range(2):

        @pl.when(inside(0, 2 * side - 1))
        def _():
            arrival = side_copy(side, rim_out.at[side], rim_in.at[side], side)
            arrival.wait_recv()
            for n in range(RIM):
                flat = rim_in[side, :, n * dates : (n + 1) * dates, :]
                flat = flat.reshape(date_parts * dates, 2 * lines).T
                place = n + side * (RIM + bins)
                z_ref[0, place, 8 : 8 + lines, :] = flat[:lines]
                z_ref[1, place, 8 : 8 + lines, :] = flat[lines:]
            arrival.wait_send()

    for step in range(chunks):
        for k in range(1, az_parts):
            az_copy(step, lax.rem(my_az + k, az_parts)).wait_send()
    for k in range(1, date_parts):
        date_arrival(lax.rem(my_date + k, date_parts)).wait_send()
    for n, (dd, da) in enumerate(neighbours()):
        if dd == 0:
            continue

        @pl.when(inside(dd, da))
        def _():
            rim_copy(n, dd, da).wait_send()

        @pl.when(inside(-dd, -da))
        def _():
            rim_copy(n, dd, da).wait_recv()


def exchange(raw, filt):
    az_parts, date_parts = lax.axis_size("az"), lax.axis_size("date")
    _, dates, all_bins, width = raw.shape
    bins, length = all_bins // az_parts, width * az_parts
    lines, radix = length // date_parts, length // LANES
    chunk = 2 if dates % 2 == 0 else 1
    forward, backward, twist = focus_tables(length)
    filt = filt.reshape(2, bins, LANES, radix).transpose(0, 3, 1, 2)
    near = pl.BlockSpec(memory_space=pltpu.VMEM)
    dma = pltpu.SemaphoreType.DMA
    return pl.pallas_call(
        functools.partial(exchange_kernel, date_parts, az_parts, chunk),
        in_specs=[pl.BlockSpec(memory_space=pl.ANY)] + [near] * 4,
        out_specs=near,
        out_shape=jax.ShapeDtypeStruct(
            (2, bins + 2 * RIM, lines + 16, date_parts * dates), jnp.float32
        ),
        scratch_shapes=[
            pltpu.VMEM((az_parts, 2, dates, bins, width), jnp.float32),
            pltpu.VMEM((date_parts, dates * bins, 2 * lines), jnp.float32),
            pltpu.VMEM((date_parts * dates * bins, 2 * lines), jnp.float32),
            pltpu.VMEM((2, date_parts, RIM * dates, 2 * lines), jnp.float32),
            pltpu.VMEM((2, date_parts, RIM * dates, 2 * lines), jnp.float32),
            dma((2,)),
            dma((dates // chunk, az_parts)),
            dma((dates // chunk, az_parts)),
            dma((date_parts,)),
            dma((date_parts,)),
            dma((8,)),
            dma((8,)),
            dma((2,)),
            dma((2,)),
        ],
        compiler_params=pltpu.CompilerParams(
            collective_id=0, has_side_effects=True, vmem_limit_bytes=40 * 1024 * 1024
        ),
        name="exchange",
    )(raw, filt, jnp.asarray(forward), jnp.asarray(backward), jnp.asarray(twist))


def link_kernel(off_ref, z_ref, s_ref, o_ref, win, mat, tam, mask):
    i, j = pl.program_id(0), pl.program_id(1)
    dates = z_ref.shape[3]

    @pl.when((i == 0) & (j == 0))
    def _():
        pixel = lax.broadcasted_iota(jnp.int32, (PIXELS, SLOTS), 0)
        slot = lax.broadcasted_iota(jnp.int32, (PIXELS, SLOTS), 1)
        line, col = pixel // TILE, pixel % TILE
        slot_col = (slot * 171) >> 11
        slot_line = slot - slot_col * SPAN_ROWS
        inside = (slot < USED) & (slot_line >= line) & (slot_line < line + WIN)
        inside = inside & (slot_col >= col) & (slot_col < col + WIN)
        one = jnp.where(inside, 1.0, 0.0)
        mask[...] = jnp.concatenate([one, one], axis=1)

    def product(value, table_ref):
        high, low = parts_of(value)
        if STACKED:
            rows, depth = value.shape
            both = jnp.dot(
                jnp.concatenate([high, low], axis=0),
                table_ref[:depth],
                preferred_element_type=jnp.float32,
            )
            rest = jnp.dot(high, table_ref[depth:], preferred_element_type=jnp.float32)
            return both[:rows] + (both[rows:] + rest)
        return jnp.dot(
            jnp.concatenate([high, low, high], axis=1),
            table_ref[...],
            preferred_element_type=jnp.float32,
        )

    def stacked(high, low):
        return jnp.concatenate([high, low] if STACKED else [high, high, low], axis=0)

    vecs, scales = [], []
    for g in range(GROUP):
        number = i * GROUP + g
        first_row = number * HALF + 9 - RIM + off_ref[number // 2, j, 0]
        first_col = j * TILE + 1 + off_ref[number // 2, j, 1]
        for c in range(2):
            for b in range(SPAN_COLS):
                win[g, c, b * SPAN_ROWS : (b + 1) * SPAN_ROWS, :] = z_ref[
                    c, first_col + b, pl.ds(first_row, SPAN_ROWS), :
                ]
            win[g, c, USED:SLOTS, :] = jnp.zeros((SLOTS - USED, dates), jnp.float32)
        zr, zi = win[g, 0], win[g, 1]
        picks = mask[...].astype(jnp.bfloat16)
        power = jnp.dot(
            picks,
            jnp.concatenate(parts_of(zr * zr + zi * zi), axis=0),
            preferred_element_type=jnp.float32,
        )
        scale = 1.0 / jnp.sqrt(power + 1e-06)
        scales.append(jnp.concatenate([scale, scale], axis=1))

        whole = jnp.concatenate(
            [jnp.concatenate([zr, zi], axis=1), jnp.concatenate([-zi, zr], axis=1)], axis=0
        )
        mat[g] = stacked(*parts_of(whole))
        tr, ti = zr.T, zi.T
        whole = jnp.concatenate(
            [jnp.concatenate([tr, -ti], axis=1), jnp.concatenate([ti, tr], axis=1)], axis=0
        )
        tam[g] = stacked(*parts_of(whole))
        rows = slice(g * HALF, (g + 1) * HALF)
        vecs.append(
            jnp.concatenate(
                [s_ref[0, rows].reshape(PIXELS, dates), s_ref[1, rows].reshape(PIXELS, dates)],
                axis=1,
            )
        )

    for step in range(ITERS):
        projs = [product(vecs[g] * scales[g], tam.at[g]) * mask[...] for g in range(GROUP)]
        for g in range(GROUP):
            gam = product(projs[g], mat.at[g]) * scales[g]
            total = jnp.sum(gam * gam, axis=1, keepdims=True) + 1e-06
            vecs[g] = gam * (1.0 / jnp.sqrt(total))
    for g in range(GROUP):
        rows = slice(g * HALF, (g + 1) * HALF)
        o_ref[0, rows] = vecs[g][:, :dates].reshape(HALF, TILE, dates)
        o_ref[1, rows] = vecs[g][:, dates:].reshape(HALF, TILE, dates)


def link(window, starts, shifts):
    _, lines, bins, dates = starts.shape
    copies = 2 if STACKED else 3
    spec = pl.BlockSpec((2, GROUP * HALF, TILE, dates), lambda i, j, off: (0, i, j, 0))
    return pl.pallas_call(
        link_kernel,
        grid_spec=pltpu.PrefetchScalarGridSpec(
            num_scalar_prefetch=1,
            grid=(lines // (GROUP * HALF), bins // TILE),
            in_specs=[pl.BlockSpec(window.shape, lambda i, j, off: (0, 0, 0, 0)), spec],
            out_specs=spec,
            scratch_shapes=[
                pltpu.VMEM((GROUP, 2, SLOTS, dates), jnp.float32),
                pltpu.VMEM((GROUP, copies * 2 * SLOTS, 2 * dates), jnp.bfloat16),
                pltpu.VMEM((GROUP, copies * 2 * dates, 2 * SLOTS), jnp.bfloat16),
                pltpu.VMEM((PIXELS, 2 * SLOTS), jnp.float32),
            ],
        ),
        out_shape=jax.ShapeDtypeStruct(starts.shape, jnp.float32),
        compiler_params=pltpu.CompilerParams(vmem_limit_bytes=40 * 1024 * 1024),
        name="link",
    )(shifts, window, starts)


def shards(raw_stack, azimuth_filter, start_vectors, window_offsets):
    bins = raw_stack.shape[2] // lax.axis_size("az")
    filt_part = lax.dynamic_slice_in_dim(azimuth_filter, lax.axis_index("az") * bins, bins, 1)
    window = exchange(raw_stack, filt_part)
    return link(window, start_vectors, window_offsets)


def solution(mesh):
    placed = (P(None, "date", None, "az"), P(), P(None, "date", "az", None), P("date", "az", None))
    return jax.shard_map(
        shards, mesh=mesh, in_specs=placed, out_specs=P(None, "date", "az", None), check_vma=False
    )
```

```python
import functools
import math

import jax
import jax.numpy as jnp
import numpy as np
from jax import lax
from jax.experimental import pallas as pl
from jax.experimental.pallas import tpu as pltpu
from jax.sharding import PartitionSpec as P

TILE = 16
WIN = 5
ITERS = 8
RIM = WIN // 2 + 1
HALF = TILE // 2
SPAN_ROWS = HALF + WIN - 1
SPAN_COLS = TILE + WIN - 1
PIXELS = HALF * TILE
USED = SPAN_ROWS * SPAN_COLS
SLOTS = 256
LANES = 128
GROUP = 8
STACKED = False


def parts_of(value):
    high = value.astype(jnp.bfloat16)
    return high, (value - high.astype(jnp.float32)).astype(jnp.bfloat16)


def butterflies(values, sign):
    count = len(values)
    if count == 1:
        return values
    even = butterflies(values[0::2], sign)
    odd = butterflies(values[1::2], sign)
    low, high = [], []
    for k in range(count // 2):
        (er, ei), (dr, di) = even[k], odd[k]
        if k == 0:
            tr, ti = dr, di
        elif 4 * k == count:
            tr, ti = (-di, dr) if sign > 0 else (di, -dr)
        else:
            c = math.cos(2 * math.pi * k / count)
            s = sign * math.sin(2 * math.pi * k / count)
            tr, ti = dr * c - di * s, dr * s + di * c
        low.append((er + tr, ei + ti))
        high.append((er - tr, ei - ti))
    return low + high


def focus_tables(length):
    radix = length // LANES
    a = np.arange(LANES)
    angle = 2 * np.pi * (np.outer(a, a) % LANES) / LANES
    c, s = np.cos(angle), np.sin(angle)
    forward = np.block([[c, -s], [s, c]])
    backward = np.block([[c, s], [-s, c]])

    def stacked(table):
        high = table.astype(jnp.bfloat16)
        low = (table - high.astype(np.float64)).astype(jnp.bfloat16)
        return np.concatenate([high, high, low], axis=0)

    turn = 2 * np.pi * np.outer(np.arange(radix), a) / length
    twist = np.stack([np.cos(turn), np.sin(turn)]).astype(np.float32)
    return stacked(forward), stacked(backward), twist


def neighbours():
    return [(dd, da) for dd in (-1, 0, 1) for da in (-1, 0, 1) if (dd, da) != (0, 0)]


def exchange_kernel(
    date_parts, az_parts, chunk,
    raw_ref, f_ref, fwd_ref, bwd_ref, tw_ref, z_ref,
    inbox, outbox, mailbox, rim_out, rim_in,
    own_sem, az_send, az_recv, date_send, date_recv, rim_send, rim_recv, x_send, x_recv,
):
    _, dates, all_bins, width = raw_ref.shape
    bins = all_bins // az_parts
    length = width * az_parts
    lines = length // date_parts
    radix = length // LANES
    chunks = dates // chunk
    rows = chunk * bins
    block = dates * bins
    my_date, my_az = lax.axis_index("date"), lax.axis_index("az")

    def inside(dd, da):
        date, az = my_date + dd, my_az + da
        return (date >= 0) & (date < date_parts) & (az >= 0) & (az < az_parts)

    def device(date, az):
        return {"date": date, "az": az}

    z_ref[...] = jnp.zeros_like(z_ref)
    barrier = pltpu.get_barrier_semaphore()
    mesh_ids = pl.DeviceIdType.MESH
    expected = date_parts - 1 + az_parts - 1
    for k in range(1, date_parts):
        peer = lax.rem(my_date + k, date_parts)
        pl.semaphore_signal(barrier, inc=1, device_id=device(peer, my_az), device_id_type=mesh_ids)
    for k in range(1, az_parts):
        peer = lax.rem(my_az + k, az_parts)
        pl.semaphore_signal(barrier, inc=1, device_id=device(my_date, peer), device_id_type=mesh_ids)
    for dd, da in neighbours():
        if dd != 0 and da != 0:
            there = inside(dd, da)
            expected = expected + there.astype(jnp.int32)

            @pl.when(there)
            def _():
                pl.semaphore_signal(
                    barrier,
                    inc=1,
                    device_id=device(my_date + dd, my_az + da),
                    device_id_type=mesh_ids,
                )

    pl.semaphore_wait(barrier, expected)

    def az_copy(step, peer):
        return pltpu.make_async_remote_copy(
            src_ref=raw_ref.at[
                :, pl.ds(step * chunk, chunk), pl.ds(pl.multiple_of(peer * bins, 8), bins), :
            ],
            dst_ref=inbox.at[my_az, :, pl.ds(step * chunk, chunk)],
            send_sem=az_send.at[step, peer],
            recv_sem=az_recv.at[step, my_az],
            device_id=device(my_date, peer),
            device_id_type=mesh_ids,
        )

    def az_arrival(step, peer):
        return pltpu.make_async_remote_copy(
            src_ref=raw_ref.at[:, pl.ds(step * chunk, chunk), pl.ds(0, bins), :],
            dst_ref=inbox.at[peer, :, pl.ds(step * chunk, chunk)],
            send_sem=az_send.at[step, peer],
            recv_sem=az_recv.at[step, peer],
            device_id=device(my_date, peer),
            device_id_type=mesh_ids,
        )

    for step in range(chunks):
        for k in range(1, az_parts):
            az_copy(step, lax.rem(my_az + k, az_parts)).start()
    own = pltpu.make_async_copy(
        raw_ref.at[:, :, pl.ds(pl.multiple_of(my_az * bins, 8), bins), :],
        inbox.at[my_az],
        own_sem.at[0],
    )
    own.start()
    own.wait()

    def product(value, table_ref):
        high, low = parts_of(value)
        return jnp.dot(
            jnp.concatenate([high, low, high], axis=1),
            table_ref[...],
            preferred_element_type=jnp.float32,
        )

    def date_copy(peer, start, size):
        return pltpu.make_async_remote_copy(
            src_ref=outbox.at[peer, pl.ds(start, size), :],
            dst_ref=mailbox.at[pl.ds(pl.multiple_of(my_date * block + start, 8), size), :],
            send_sem=date_send.at[peer],
            recv_sem=date_recv.at[my_date],
            device_id=device(peer, my_az),
            device_id_type=mesh_ids,
        )

    def date_arrival(peer):
        return pltpu.make_async_remote_copy(
            src_ref=outbox.at[peer],
            dst_ref=mailbox.at[pl.ds(pl.multiple_of(peer * block, 8), block), :],
            send_sem=date_send.at[peer],
            recv_sem=date_recv.at[peer],
            device_id=device(peer, my_az),
            device_id_type=mesh_ids,
        )

    @pl.loop(0, chunks)
    def _(step):
        for k in range(1, az_parts):
            az_arrival(step, lax.rem(my_az + k, az_parts)).wait_recv()
        field = []
        for b in range(radix):
            source, at = b * LANES // width, b * LANES % width
            field.append(
                tuple(
                    inbox[source, c, pl.ds(step * chunk, chunk), :, at : at + LANES].reshape(
                        rows, LANES
                    )
                    for c in range(2)
                )
            )
        stack = []
        for k, (re, im) in enumerate(butterflies(field, -1)):
            c, s = tw_ref[0, k : k + 1, :], tw_ref[1, k : k + 1, :]
            stack.append(jnp.concatenate([re * c + im * s, im * c - re * s], axis=1))
        spec = product(jnp.concatenate(stack, axis=0), fwd_ref)
        sr, si = spec[:, :LANES], spec[:, LANES:]
        full = (radix, chunk, bins, LANES)
        fr = jnp.broadcast_to(f_ref[0][:, None], full).reshape(radix * rows, LANES)
        fi = jnp.broadcast_to(f_ref[1][:, None], full).reshape(radix * rows, LANES)
        back = product(jnp.concatenate([sr * fr - si * fi, sr * fi + si * fr], axis=1), bwd_ref)
        inverse = 1.0 / length
        field = []
        for k in range(radix):
            c, s = tw_ref[0, k : k + 1, :] * inverse, tw_ref[1, k : k + 1, :] * inverse
            re = back[k * rows : (k + 1) * rows, :LANES]
            im = back[k * rows : (k + 1) * rows, LANES:]
            field.append((re * c - im * s, im * c + re * s))
        field = butterflies(field, 1)
        start = pl.multiple_of(step * rows, 8)
        for place in range(date_parts):
            b, low = place * lines // LANES, place * lines % LANES
            re, im = field[b]
            outbox[place, pl.ds(start, rows), :] = jnp.concatenate(
                [re[:, low : low + lines], im[:, low : low + lines]], axis=1
            )
        for k in range(1, date_parts):
            date_copy(lax.rem(my_date + k, date_parts), start, rows).start()

    keep = pltpu.make_async_copy(
        outbox.at[my_date],
        mailbox.at[pl.ds(pl.multiple_of(my_date * block, 8), block), :],
        own_sem.at[1],
    )
    keep.start()

    def side_copy(side, out, into, landing):
        return pltpu.make_async_remote_copy(
            src_ref=out,
            dst_ref=into,
            send_sem=x_send.at[side],
            recv_sem=x_recv.at[landing],
            device_id=device(my_date, my_az + 2 * side - 1),
            device_id_type=mesh_ids,
        )

    def forward(source):
        for side in range(2):

            @pl.when(inside(0, 2 * side - 1))
            def _():
                for n in range(RIM):
                    b = n + side * (bins - RIM)
                    rim_out[side, source, n * dates : (n + 1) * dates, :] = mailbox[
                        pl.ds(source * block + b, dates, stride=bins), :
                    ]
                side_copy(
                    side, rim_out.at[side, source], rim_in.at[1 - side, source], 1 - side
                ).start()

    keep.wait()
    forward(my_date)
    for k in range(1, date_parts):
        shift = (k + 1) // 2 if k % 2 else date_parts - k // 2
        peer = lax.rem(my_date + shift, date_parts)
        date_arrival(peer).wait_recv()
        forward(peer)

    def rim_copy(n, dd, da):
        lines_at = {-1: (8, 8 + lines, 8), 0: (8, 8, lines), 1: (lines, 0, 8)}[dd]
        bins_at = {-1: (RIM, RIM + bins, RIM), 0: (RIM, RIM, bins), 1: (bins, 0, RIM)}[da]
        return pltpu.make_async_remote_copy(
            src_ref=z_ref.at[:, pl.ds(bins_at[0], bins_at[2]), pl.ds(lines_at[0], lines_at[2]), :],
            dst_ref=z_ref.at[:, pl.ds(bins_at[1], bins_at[2]), pl.ds(lines_at[1], lines_at[2]), :],
            send_sem=rim_send.at[n],
            recv_sem=rim_recv.at[n],
            device_id=device(my_date + dd, my_az + da),
            device_id_type=mesh_ids,
        )

    def send_rims(side):
        for n, (dd, da) in enumerate(neighbours()):
            if da == side and dd != 0:

                @pl.when(inside(dd, da))
                def _():
                    rim_copy(n, dd, da).start()

    edge = list(range(RIM)) + list(range(bins - RIM, bins)) + list(range(RIM, bins - RIM))
    for count, b in enumerate(edge):
        flat = mailbox[pl.ds(b, date_parts * dates, stride=bins), :].T
        z_ref[0, RIM + b, 8 : 8 + lines, :] = flat[:lines]
        z_ref[1, RIM + b, 8 : 8 + lines, :] = flat[lines:]
        if count == RIM - 1:
            send_rims(-1)
        if count == 2 * RIM - 1:
            send_rims(1)
    send_rims(0)
    for side in range(2):

        @pl.when(inside(0, 2 * side - 1))
        def _():
            arrival = side_copy(side, rim_out.at[side], rim_in.at[side], side)
            arrival.wait_recv()
            for n in range(RIM):
                flat = rim_in[side, :, n * dates : (n + 1) * dates, :]
                flat = flat.reshape(date_parts * dates, 2 * lines).T
                place = n + side * (RIM + bins)
                z_ref[0, place, 8 : 8 + lines, :] = flat[:lines]
                z_ref[1, place, 8 : 8 + lines, :] = flat[lines:]
            arrival.wait_send()

    for step in range(chunks):
        for k in range(1, az_parts):
            az_copy(step, lax.rem(my_az + k, az_parts)).wait_send()
    for k in range(1, date_parts):
        date_arrival(lax.rem(my_date + k, date_parts)).wait_send()
    for n, (dd, da) in enumerate(neighbours()):
        if dd == 0:
            continue

        @pl.when(inside(dd, da))
        def _():
            rim_copy(n, dd, da).wait_send()

        @pl.when(inside(-dd, -da))
        def _():
            rim_copy(n, dd, da).wait_recv()


def exchange(raw, filt):
    az_parts, date_parts = lax.axis_size("az"), lax.axis_size("date")
    _, dates, all_bins, width = raw.shape
    bins, length = all_bins // az_parts, width * az_parts
    lines, radix = length // date_parts, length // LANES
    chunk = 2 if dates % 2 == 0 else 1
    forward, backward, twist = focus_tables(length)
    filt = filt.reshape(2, bins, LANES, radix).transpose(0, 3, 1, 2)
    near = pl.BlockSpec(memory_space=pltpu.VMEM)
    dma = pltpu.SemaphoreType.DMA
    return pl.pallas_call(
        functools.partial(exchange_kernel, date_parts, az_parts, chunk),
        in_specs=[pl.BlockSpec(memory_space=pl.ANY)] + [near] * 4,
        out_specs=near,
        out_shape=jax.ShapeDtypeStruct(
            (2, bins + 2 * RIM, lines + 16, date_parts * dates), jnp.float32
        ),
        scratch_shapes=[
            pltpu.VMEM((az_parts, 2, dates, bins, width), jnp.float32),
            pltpu.VMEM((date_parts, dates * bins, 2 * lines), jnp.float32),
            pltpu.VMEM((date_parts * dates * bins, 2 * lines), jnp.float32),
            pltpu.VMEM((2, date_parts, RIM * dates, 2 * lines), jnp.float32),
            pltpu.VMEM((2, date_parts, RIM * dates, 2 * lines), jnp.float32),
            dma((2,)),
            dma((dates // chunk, az_parts)),
            dma((dates // chunk, az_parts)),
            dma((date_parts,)),
            dma((date_parts,)),
            dma((8,)),
            dma((8,)),
            dma((2,)),
            dma((2,)),
        ],
        compiler_params=pltpu.CompilerParams(
            collective_id=0, has_side_effects=True, vmem_limit_bytes=40 * 1024 * 1024
        ),
        name="exchange",
    )(raw, filt, jnp.asarray(forward), jnp.asarray(backward), jnp.asarray(twist))


def link_kernel(off_ref, z_ref, s_ref, o_ref, win, mat, tam, mask):
    i, j = pl.program_id(0), pl.program_id(1)
    dates, group = z_ref.shape[3], s_ref.shape[1] // HALF

    @pl.when((i == 0) & (j == 0))
    def _():
        pixel = lax.broadcasted_iota(jnp.int32, (PIXELS, SLOTS), 0)
        slot = lax.broadcasted_iota(jnp.int32, (PIXELS, SLOTS), 1)
        line, col = pixel // TILE, pixel % TILE
        slot_col = (slot * 171) >> 11
        slot_line = slot - slot_col * SPAN_ROWS
        inside = (slot < USED) & (slot_line >= line) & (slot_line < line + WIN)
        inside = inside & (slot_col >= col) & (slot_col < col + WIN)
        one = jnp.where(inside, 1.0, 0.0)
        mask[...] = jnp.concatenate([one, one], axis=1)

    def product(value, table_ref):
        high, low = parts_of(value)
        if STACKED:
            rows, depth = value.shape
            both = jnp.dot(
                jnp.concatenate([high, low], axis=0),
                table_ref[:depth],
                preferred_element_type=jnp.float32,
            )
            rest = jnp.dot(high, table_ref[depth:], preferred_element_type=jnp.float32)
            return both[:rows] + (both[rows:] + rest)
        return jnp.dot(
            jnp.concatenate([high, low, high], axis=1),
            table_ref[...],
            preferred_element_type=jnp.float32,
        )

    def stacked(high, low):
        return jnp.concatenate([high, low] if STACKED else [high, high, low], axis=0)

    vecs, scales = [], []
    for g in range(group):
        number = i * group + g
        first_row = number * HALF + 9 - RIM + off_ref[number // 2, j, 0]
        first_col = j * TILE + 1 + off_ref[number // 2, j, 1]
        for c in range(2):
            for b in range(SPAN_COLS):
                win[g, c, b * SPAN_ROWS : (b + 1) * SPAN_ROWS, :] = z_ref[
                    c, first_col + b, pl.ds(first_row, SPAN_ROWS), :
                ]
            win[g, c, USED:SLOTS, :] = jnp.zeros((SLOTS - USED, dates), jnp.float32)
        zr, zi = win[g, 0], win[g, 1]
        picks = mask[...].astype(jnp.bfloat16)
        power = jnp.dot(
            picks,
            jnp.concatenate(parts_of(zr * zr + zi * zi), axis=0),
            preferred_element_type=jnp.float32,
        )
        scale = 1.0 / jnp.sqrt(power + 1e-06)
        scales.append(jnp.concatenate([scale, scale], axis=1))

        whole = jnp.concatenate(
            [jnp.concatenate([zr, zi], axis=1), jnp.concatenate([-zi, zr], axis=1)], axis=0
        )
        mat[g] = stacked(*parts_of(whole))
        tr, ti = zr.T, zi.T
        whole = jnp.concatenate(
            [jnp.concatenate([tr, -ti], axis=1), jnp.concatenate([ti, tr], axis=1)], axis=0
        )
        tam[g] = stacked(*parts_of(whole))
        rows = slice(g * HALF, (g + 1) * HALF)
        vecs.append(
            jnp.concatenate(
                [s_ref[0, rows].reshape(PIXELS, dates), s_ref[1, rows].reshape(PIXELS, dates)],
                axis=1,
            )
        )

    for step in range(ITERS):
        projs = [product(vecs[g] * scales[g], tam.at[g]) * mask[...] for g in range(group)]
        for g in range(group):
            gam = product(projs[g], mat.at[g]) * scales[g]
            total = jnp.sum(gam * gam, axis=1, keepdims=True) + 1e-06
            vecs[g] = gam * (1.0 / jnp.sqrt(total))
    for g in range(group):
        rows = slice(g * HALF, (g + 1) * HALF)
        o_ref[0, rows] = vecs[g][:, :dates].reshape(HALF, TILE, dates)
        o_ref[1, rows] = vecs[g][:, dates:].reshape(HALF, TILE, dates)


def link(window, starts, shifts):
    _, lines, bins, dates = starts.shape
    copies = 2 if STACKED else 3
    group = math.gcd(GROUP, lines // HALF)
    spec = pl.BlockSpec((2, group * HALF, TILE, dates), lambda i, j, off: (0, i, j, 0))
    return pl.pallas_call(
        link_kernel,
        grid_spec=pltpu.PrefetchScalarGridSpec(
            num_scalar_prefetch=1,
            grid=(lines // (group * HALF), bins // TILE),
            in_specs=[pl.BlockSpec(window.shape, lambda i, j, off: (0, 0, 0, 0)), spec],
            out_specs=spec,
            scratch_shapes=[
                pltpu.VMEM((group, 2, SLOTS, dates), jnp.float32),
                pltpu.VMEM((group, copies * 2 * SLOTS, 2 * dates), jnp.bfloat16),
                pltpu.VMEM((group, copies * 2 * dates, 2 * SLOTS), jnp.bfloat16),
                pltpu.VMEM((PIXELS, 2 * SLOTS), jnp.float32),
            ],
        ),
        out_shape=jax.ShapeDtypeStruct(starts.shape, jnp.float32),
        compiler_params=pltpu.CompilerParams(vmem_limit_bytes=40 * 1024 * 1024),
        name="link",
    )(shifts, window, starts)


def shards(raw_stack, azimuth_filter, start_vectors, window_offsets):
    bins = raw_stack.shape[2] // lax.axis_size("az")
    filt_part = lax.dynamic_slice_in_dim(azimuth_filter, lax.axis_index("az") * bins, bins, 1)
    window = exchange(raw_stack, filt_part)
    return link(window, start_vectors, window_offsets)


def solution(mesh):
    placed = (P(None, "date", None, "az"), P(), P(None, "date", "az", None), P("date", "az", None))
    return jax.shard_map(
        shards, mesh=mesh, in_specs=placed, out_specs=P(None, "date", "az", None), check_vma=False
    )
```
